32 devices in a mesh: tm: 4 (over x, core), mem: 8 (over z, y).
Axes of the slice: x: 2, y: 2, z: 4, core: 2. Of those that a mesh axis runs over, the one named last changes fastest.
Arguments:
- tokens: bfloat16 [8192, 2048], P(('tm', 'mem')), may hold values from -6 to 6
- queries: bfloat16 [8192, 2048], P(('tm', 'mem')), may hold values from -6 to 6
- log_decay: bfloat16 [8192, 16], P(('tm', 'mem')), may hold values from -1 to 0
- route_ids: int32 [8192, 2], P(('tm', 'mem')), may hold values from 0 to 7, all different within a row; in each aligned block of 256 rows (0 to 255, 256 to 511, ...) at most 96 rows name the same one
- gate_weights: float32 [8192, 2], P(('tm', 'mem')), may hold values from 0.3 to 1
- kv_weight: bfloat16 [8, 2048, 4096], P('mem'), may hold values from -0.125 to 0.125
Outputs:
- mixed: bfloat16 [8192, 2048], P(('tm', 'mem'))
The draws below stay inside these ranges and needn't reach their ends.
Inputs may be any that keep to these rules, and one draw needn't show every extreme that they name: `route_ids`: each row names 2 different memories. In each aligned block of 256 rows (the rows of one device) no memory is named by more than 96 rows, and in some block one memory is named by exactly 96 rows.
All inputs are finite; a program needn't handle non-finite values.
Results may differ from the reference program's by a relative error of at most 0.006.
Values may be sent and summed in bfloat16 or wider, within the bound.
No kernel may reach another device: no remote copies, remote signals or barrier semaphores. Data moves between devices by JAX's collectives and lax.ppermute only.
A program may use at most 128 MiB of HBM per device.

```python
import math
import jax
import jax.numpy as jnp
import numpy as np
from jax import lax

D = 2048
H = 16
HD = 128
TOP = 2
TOK_DEV = 256
STATE_COUNT = 8
WORD_COUNT = 8192
CAP = 96
N_TM = 4
N_MEM = 8


def draw_log_decay(key, part):
    derived_seed_list = jax.random.split(key, 7)
    chain_mean = WORD_COUNT * TOP / STATE_COUNT
    slow_heads = jax.random.uniform(derived_seed_list[0], (H,)) < 0.5
    fast_rate = jnp.exp(jax.random.uniform(derived_seed_list[1], (H,), minval=math.log(1.0 / 50.0), maxval=math.log(1.0 / 30.0)))
    slow_rate = jnp.exp(jax.random.uniform(derived_seed_list[2], (H,), minval=math.log(0.2), maxval=0.0)) / chain_mean
    rates = jnp.where(slow_heads, slow_rate, fast_rate)
    rough = jnp.exp(jax.random.uniform(derived_seed_list[3], (WORD_COUNT, H), minval=-math.log(2.0), maxval=math.log(2.0)))
    device_factor = jnp.exp(jax.random.uniform(derived_seed_list[4], (WORD_COUNT // TOK_DEV, 1, H), minval=-math.log(2.0), maxval=math.log(2.0)))
    starting_shift = -(rates[None, :] * rough).reshape(WORD_COUNT // TOK_DEV, TOK_DEV, H) * device_factor
    starting_shift = starting_shift.reshape(WORD_COUNT, H)
    span_extent = jax.random.randint(derived_seed_list[5], (WORD_COUNT, 1), 0, WORD_COUNT) < max(STATE_COUNT // 2, 1)
    stack_level = jax.random.uniform(derived_seed_list[6], (WORD_COUNT, H), minval=math.log(0.5), maxval=math.log(0.8))
    emitted_result = starting_shift + jnp.where(span_extent, stack_level, 0.0)
    return emitted_result.astype(jnp.float32).astype(jnp.bfloat16)


def level_of(own_key, extent, cuts, smallest, top_value):
    gain, own = 1.0, jax.random.fold_in(own_key, 6)
    for dim, blocks in cuts:
        heights = jnp.exp(jax.random.uniform(jax.random.fold_in(own, dim), (blocks,), jnp.float32, smallest / len(cuts), top_value / len(cuts)))
        gain = gain * jnp.repeat(heights, extent[dim] // blocks).reshape([-1 if axis == dim else 1 for axis in range(len(extent))])
    return gain


def routed_block(rng, own, number, rows, amount, top, limit, slope):
    ranking = jax.random.permutation(rng, amount)
    crowded, common = load_shares(amount, rows * top, limit, slope, True), load_shares(amount, rows * top, limit, slope, False)
    places = jnp.arange(amount)

    def named(lengths, turn):
        used = int((lengths > 0).sum())
        fixed = max(1, used // 4)
        moved = fixed + (places - fixed + turn * (used - fixed)) % max(1, amount - fixed)
        return jnp.zeros((amount,), jnp.int32).at[ranking[jnp.where(places < fixed, places, moved)]].set(jnp.asarray(lengths, jnp.int32))

    lengths = jnp.where(number % 4 == 0, named(crowded, number // 4), named(common, number - number // 4 - 1))
    mixed = jax.random.permutation(jax.random.fold_in(own, 3), amount)
    giver, taker = mixed[0:amount // 2 * 2:2], mixed[1:amount // 2 * 2:2]
    margin = jnp.minimum(lengths[giver] - 1, limit - lengths[taker]) // 2
    margin = jnp.where((giver == ranking[0]) | (taker == ranking[0]) | (lengths[taker] == 0), 0, jnp.maximum(margin, 0))
    moved = jax.random.randint(jax.random.fold_in(own, 4), (amount // 2,), 0, 1 << 20) % (margin + 1)
    lengths = lengths.at[giver].add(-moved).at[taker].add(moved)
    labels = jnp.searchsorted(jnp.cumsum(lengths), jnp.arange(rows * top), side="right").astype(jnp.int32)
    grid = labels.reshape(top, rows).T
    grid = grid[jax.random.permutation(jax.random.fold_in(own, 1), rows)]
    turn = jax.random.randint(jax.random.fold_in(own, 2), (rows, 1), 0, top)
    return jnp.take_along_axis(grid, (jnp.arange(top)[None, :] + turn) % top, axis=1)


def load_shares(number_of, total, limit, skew, full):
    portions = [(1 << 20) // math.isqrt(rank ** skew) + 1 for rank in range(1, number_of + 1)]
    largest = limit if full else min(limit, max(-(-total // number_of), total * portions[0] // sum(portions)))
    least = 1 if total - largest >= number_of - 1 else 0
    counts, spare = [largest] + [least] * (number_of - 1), total - largest - least * (number_of - 1)
    while spare > 0:
        candidates = [i for i in range(1, number_of) if counts[i] < largest] or [i for i in range(1, number_of) if counts[i] < limit]
        whole, budget = sum([portions[i] for i in candidates]), spare
        for i in candidates:
            more = min(limit - counts[i], max(1, budget * portions[i] // whole), spare)
            counts[i] = counts[i] + more
            spare = spare - more
    return np.array(counts)


def centred(key, shape, scale, bound, cuts=(), kind=jnp.bfloat16):
    array = jax.random.normal(key, shape, jnp.float32) * scale
    if len(cuts) > 0:
        array = level_of(key, shape, cuts, -0.22, 0.18) * array
    return jnp.clip(array, min=-bound, max=bound).astype(kind)


def setup_inputs(seed: int = 0) -> dict:
    splits = jax.random.split(jax.random.key(seed), 7)
    tokens = centred(splits[0], (WORD_COUNT, D), 1.0, 6.0, ((0, 32),))
    queries = centred(splits[1], (WORD_COUNT, D), 1.0, 6.0, ((0, 32),))
    log_decay = draw_log_decay(jax.random.fold_in(splits[6], 71), 0)
    route_ids_keys = jax.random.split(jax.random.fold_in(splits[3], 1), WORD_COUNT // TOK_DEV)
    route_ids_turns = jax.random.permutation(jax.random.fold_in(splits[3], 3), WORD_COUNT // TOK_DEV)
    route_ids = jax.vmap(lambda own, number: routed_block(jax.random.fold_in(splits[3], 2), own, number, TOK_DEV, STATE_COUNT, TOP, CAP, 2))(route_ids_keys, route_ids_turns).reshape((WORD_COUNT, TOP))
    gate_weights = jnp.clip(0.3 + 0.7 * jax.random.uniform(splits[4], (WORD_COUNT, TOP), jnp.float32) ** level_of(splits[4], (WORD_COUNT, TOP), ((0, 32),), -0.2, 0.2), 0.3, 1.0)
    kv_weight = centred(splits[5], (STATE_COUNT, D, 2 * D), D ** -0.5, 0.125, ((0, 8),))
    return dict(tokens=tokens, queries=queries, log_decay=log_decay, route_ids=route_ids, gate_weights=gate_weights, kv_weight=kv_weight)


exact_mode = lax.Precision.HIGHEST

def block_pass(queries_heads, keys_heads, values_heads, decay_logs, block_rows):
    head_count, chain_rows, head_size = queries_heads.shape
    block_count = chain_rows // block_rows

    def split_blocks(tensor):
        return jnp.moveaxis(tensor.reshape(head_count, block_count, block_rows, head_size), 1, 0)
    blocked = (split_blocks(queries_heads), split_blocks(keys_heads), split_blocks(values_heads), jnp.moveaxis(decay_logs.reshape(head_count, block_count, block_rows), 1, 0))
    lower = jnp.arange(block_rows)[:, None] >= jnp.arange(block_rows)[None, :]

    def advance(carried, pieces):
        query_block, key_block, value_block, log_block = pieces
        running = jnp.cumsum(log_block, axis=1)
        spread = jnp.minimum(running[:, :, None] - running[:, None, :], 0.0)
        weights = jnp.where(lower[None], jnp.exp(spread), 0.0)
        scores = jnp.einsum('hnd,hid->hni', query_block, key_block, preferred_element_type=jnp.float32) * weights
        value_wide = value_block.astype(jnp.float32)
        within = jnp.einsum('hni,hie->hne', scores, value_wide, precision=exact_mode)
        earlier = jnp.einsum('hnd,hde->hne', query_block.astype(jnp.float32), carried, precision=exact_mode) * jnp.exp(running)[:, :, None]
        ending = running[:, -1]
        fading = jnp.exp(ending[:, None] - running)
        carried = jnp.exp(ending)[:, None, None] * carried + jnp.einsum('hid,hie->hde', key_block.astype(jnp.float32) * fading[:, :, None], value_wide, precision=exact_mode)
        return (carried, within + earlier)
    start = jnp.zeros((head_count, head_size, head_size), jnp.float32)
    final_state, outputs = lax.scan(advance, start, blocked)
    outputs = jnp.moveaxis(outputs, 0, 1).reshape(head_count, chain_rows, head_size)
    return (final_state, outputs)

def normalize(outputs):
    mean_square = lax.optimization_barrier(jnp.mean(outputs * outputs, axis=-1, keepdims=True))
    return outputs * lax.rsqrt(mean_square + 1e-06)

def reference(tokens, queries, log_decay, route_ids, gate_weights, kv_weight):
    chain_len = N_TM * N_MEM * CAP
    block_rows = math.gcd(chain_len, 512)
    positions = jnp.arange(WORD_COUNT, dtype=jnp.int32)

    def one_memory(total, memory):
        named = route_ids == memory
        routed = jnp.any(named, axis=1)
        order_key = jnp.where(routed, positions, WORD_COUNT + positions).astype(jnp.int32)
        picked = jnp.argsort(order_key)[:chain_len].astype(jnp.int32)
        valid = routed[picked]
        chain_x = jnp.where(valid[:, None], tokens[picked], jnp.zeros((), jnp.bfloat16))
        weight_now = lax.dynamic_index_in_dim(kv_weight, memory, 0, keepdims=False)
        projected = jnp.dot(chain_x, weight_now, preferred_element_type=jnp.float32).astype(jnp.bfloat16)
        keys_heads = projected[:, :D].reshape(chain_len, H, HD).transpose(1, 0, 2)
        values_heads = projected[:, D:].reshape(chain_len, H, HD).transpose(1, 0, 2)
        query_heads = queries[picked].reshape(chain_len, H, HD).transpose(1, 0, 2)
        logs_heads = jnp.where(valid[:, None], log_decay[picked].astype(jnp.float32), 0.0).T
        final_state, outputs = block_pass(query_heads, keys_heads, values_heads, logs_heads, block_rows)
        normed = normalize(outputs).astype(jnp.bfloat16).transpose(1, 0, 2).reshape(chain_len, D)
        gate_here = lax.optimization_barrier(jnp.sum(jnp.where(named, gate_weights, 0.0), axis=1))[picked]
        gate_here = jnp.where(valid, gate_here, 0.0)
        total = total.at[picked].add(gate_here[:, None] * normed.astype(jnp.float32))
        return (total, None)
    start = jnp.zeros((WORD_COUNT, D), jnp.float32)
    total, unused = lax.scan(one_memory, start, jnp.arange(STATE_COUNT, dtype=jnp.int32))
    return total.astype(jnp.bfloat16)
```

```python
import math

import jax
import jax.numpy as jnp
from jax import lax
from jax.experimental import pallas as pl
from jax.experimental.pallas import tpu as pltpu
from jax.sharding import PartitionSpec as P

F32 = jnp.float32
BF16 = jnp.bfloat16
VMEM_LIMIT = 40 << 20


def mm(a, b):
    return lax.dot_general(a, b, (((1,), (0,)), ((), ())), preferred_element_type=F32)


def mm_nt(a, b):
    return lax.dot_general(a, b, (((1,), (1,)), ((), ())), preferred_element_type=F32)


def split(x):
    high = x.astype(BF16)
    return high, (x - high.astype(F32)).astype(BF16)


def row_slots(routes, members, capacity):
    top, rows = routes.shape
    member = lax.broadcasted_iota(jnp.int32, (members, rows), 0)
    hits = [routes[j : j + 1, :] == member for j in range(top)]
    named = hits[0]
    for h in hits[1:]:
        named = jnp.logical_or(named, h)
    source = lax.broadcasted_iota(jnp.int32, (rows, rows), 0)
    target = lax.broadcasted_iota(jnp.int32, (rows, rows), 1)
    earlier = jnp.where(source < target, 1.0, 0.0).astype(BF16)
    before = mm(jnp.where(named, 1.0, 0.0).astype(BF16), earlier)
    slots = []
    for j in range(top):
        place = jnp.sum(jnp.where(hits[j], before, 0.0), axis=0, keepdims=True)
        slots.append(routes[j : j + 1, :] * capacity + place.astype(jnp.int32))
    return slots


def selection(routes, members, capacity):
    rows = routes.shape[1]
    slots = row_slots(routes, members, capacity)
    index = lax.broadcasted_iota(jnp.int32, (members * capacity, rows), 0)
    chosen = index == slots[0]
    for s in slots[1:]:
        chosen = jnp.logical_or(chosen, index == s)
    return jnp.where(chosen, 1.0, 0.0).astype(BF16)


def dispatch(routes_t, data, members, capacity, parts, decay=None):
    rows, width = data.shape
    chain = members * capacity
    part = width // parts
    tile = min(512, part)
    steps = width // tile
    per = part // tile

    def kernel(*refs):
        if decay is not None:
            routes_ref, data_ref, decay_ref = refs[:3]
            outs, decay_out, pick = refs[3 : 3 + parts], refs[3 + parts], refs[-1]
        else:
            routes_ref, data_ref = refs[:2]
            outs, pick = refs[2 : 2 + parts], refs[-1]
        step = pl.program_id(0)

        @pl.when(step == 0)
        def _():
            chosen = selection(routes_ref[...], members, capacity)
            pick[...] = chosen
            if decay is not None:
                picked = mm_nt(decay_ref[...], chosen).astype(BF16)
                for e in range(members):
                    decay_out[e] = picked[:, e * capacity : (e + 1) * capacity]

        rows_out = mm(pick[...], data_ref[...]).astype(BF16)
        for p in range(parts):

            @pl.when(step // per == p)
            def _():
                outs[p][...] = rows_out

    in_specs = [
        pl.BlockSpec(routes_t.shape, lambda i: (0, 0)),
        pl.BlockSpec((rows, tile), lambda i: (0, i)),
    ]
    args = [routes_t, data]
    out_shape = [jax.ShapeDtypeStruct((chain, part), BF16) for _ in range(parts)]
    out_specs = [
        pl.BlockSpec((chain, tile), lambda i, p=p: (0, jnp.clip(i - p * per, 0, per - 1)))
        for p in range(parts)
    ]
    if decay is not None:
        heads = decay.shape[0]
        in_specs.append(pl.BlockSpec(decay.shape, lambda i: (0, 0)))
        args.append(decay)
        out_shape.append(jax.ShapeDtypeStruct((members, heads, capacity), BF16))
        out_specs.append(pl.BlockSpec((members, heads, capacity), lambda i: (0, 0, 0)))
    return pl.pallas_call(
        kernel,
        grid=(steps,),
        in_specs=in_specs,
        out_specs=out_specs,
        out_shape=out_shape,
        scratch_shapes=[pltpu.VMEM((chain, rows), BF16)],
        compiler_params=pltpu.CompilerParams(vmem_limit_bytes=VMEM_LIMIT),
        cost_estimate=pl.CostEstimate(
            flops=2 * chain * rows * width,
            bytes_accessed=2 * width * (rows + chain),
            transcendentals=0,
        ),
    )(*args)


def local_states(projected, running, head_count, head_size):
    chain = projected.shape[0]

    def kernel(keys_ref, values_ref, running_ref, state_ref):
        h = pl.program_id(0)

        @pl.when(h < head_count)
        def _():
            row = running_ref[pl.ds(h, 1), :]
            fade = jnp.exp(row[:, chain - 1 :] - row)
            faded = keys_ref[...].T.astype(F32) * fade
            high, low = split(faded)
            values = values_ref[...]
            state_ref[0] = mm(high, values) + mm(low, values)

        @pl.when(h == head_count)
        def _():
            state_ref[...] = jnp.zeros_like(state_ref)
            state_ref[0, :head_count, :] = jnp.broadcast_to(
                running_ref[:, chain - 1 :], (head_count, head_size)
            )

    last = head_count - 1
    return pl.pallas_call(
        kernel,
        grid=(head_count + 1,),
        in_specs=[
            pl.BlockSpec((chain, head_size), lambda h: (0, jnp.minimum(h, last))),
            pl.BlockSpec((chain, head_size), lambda h: (0, head_count + jnp.minimum(h, last))),
            pl.BlockSpec(running.shape, lambda h: (0, 0)),
        ],
        out_specs=pl.BlockSpec((1, head_size, head_size), lambda h: (h, 0, 0)),
        out_shape=jax.ShapeDtypeStruct((head_count + 1, head_size, head_size), F32),
        compiler_params=pltpu.CompilerParams(vmem_limit_bytes=VMEM_LIMIT),
        cost_estimate=pl.CostEstimate(
            flops=4 * chain * head_size * head_size * head_count,
            bytes_accessed=projected.size * 2 + head_count * head_size * head_size * 4,
            transcendentals=chain * head_count,
        ),
    )(projected, projected, running)


def chain_outputs(queries, projected, running, incoming, first_head, head_count, head_size, rows):
    chain, width = queries.shape
    here = width // head_size

    def kernel(queries_ref, keys_ref, values_ref, running_ref, incoming_ref, out_ref):
        h = pl.program_id(0) + first_head
        state = incoming_ref[0]
        running_row = running_ref[pl.ds(h, 1), :]
        up = lax.broadcasted_iota(jnp.int32, (rows, rows), 0)
        across = lax.broadcasted_iota(jnp.int32, (rows, rows), 1)
        lower = up >= across
        previous = jnp.zeros((1, 1), F32)
        for c in range(chain // rows):
            span = slice(c * rows, (c + 1) * rows)
            query, key, value = queries_ref[span, :], keys_ref[span, :], values_ref[span, :]
            row = running_row[:, span]
            wide = jnp.broadcast_to(row, (rows, rows))
            tall = wide.T
            weights = jnp.where(lower, jnp.exp(jnp.minimum(tall - wide, 0.0)), 0.0)
            scores, scores_low = split(mm_nt(query, key) * weights)
            state_high, state_low = split(state)
            grown = jnp.exp(tall[:, :head_size] - previous)
            earlier = (mm(query, state_high) + mm(query, state_low)) * grown
            outputs = mm(scores, value) + mm(scores_low, value) + earlier
            mean_square = jnp.mean(outputs * outputs, axis=-1, keepdims=True)
            out_ref[span, :] = (outputs * lax.rsqrt(mean_square + 1e-06)).astype(BF16)
            ending = row[:, rows - 1 :]
            if (c + 1) * rows < chain:
                faded, faded_low = split(key.T.astype(F32) * jnp.exp(ending - row))
                state = (
                    jnp.exp(ending - previous) * state + mm(faded, value) + mm(faded_low, value)
                )
            previous = ending

    return pl.pallas_call(
        kernel,
        grid=(here,),
        in_specs=[
            pl.BlockSpec((chain, head_size), lambda h: (0, h)),
            pl.BlockSpec((chain, head_size), lambda h: (0, first_head + h)),
            pl.BlockSpec((chain, head_size), lambda h: (0, head_count + first_head + h)),
            pl.BlockSpec(running.shape, lambda h: (0, 0)),
            pl.BlockSpec((1, head_size, head_size), lambda h: (first_head + h, 0, 0)),
        ],
        out_specs=pl.BlockSpec((chain, head_size), lambda h: (0, h)),
        out_shape=jax.ShapeDtypeStruct((chain, width), BF16),
        compiler_params=pltpu.CompilerParams(vmem_limit_bytes=VMEM_LIMIT),
        cost_estimate=pl.CostEstimate(
            flops=here * chain * head_size * (6 * rows + 8 * head_size),
            bytes_accessed=8 * chain * width,
            transcendentals=here * chain * rows,
        ),
    )(queries, projected, projected, running, incoming)


def combine(route_ids, gate_weights, returned, mixed, part, parts, members, capacity):
    rows, top = route_ids.shape
    chain, width = returned.shape
    tile = min(512, width)
    steps = width // tile

    def kernel(*refs):
        routes_ref, gates_ref, returned_ref = refs[:3]
        out_ref, high_ref, low_ref = refs[-3:]

        @pl.when(pl.program_id(0) == 0)
        def _():
            routes = routes_ref[...]
            member = lax.broadcasted_iota(jnp.int32, (rows, members), 1)
            hits = [routes[:, j : j + 1] == member for j in range(top)]
            named = hits[0]
            for hit in hits[1:]:
                named = jnp.logical_or(named, hit)
            target = lax.broadcasted_iota(jnp.int32, (rows, rows), 0)
            source = lax.broadcasted_iota(jnp.int32, (rows, rows), 1)
            earlier = jnp.where(source < target, 1.0, 0.0).astype(BF16)
            before = mm(earlier, jnp.where(named, 1.0, 0.0).astype(BF16))
            index = lax.broadcasted_iota(jnp.int32, (rows, chain), 1)
            gates = jnp.zeros((rows, chain), F32)
            for j in range(top):
                place = jnp.sum(jnp.where(hits[j], before, 0.0), axis=1, keepdims=True)
                slot = routes[:, j : j + 1] * capacity + place.astype(jnp.int32)
                gates = jnp.where(index == slot, gates_ref[:, j : j + 1], gates)
            high_ref[...], low_ref[...] = split(gates)

        data = returned_ref[...]
        out_ref[...] = (mm(high_ref[...], data) + mm(low_ref[...], data)).astype(BF16)

    in_specs = [
        pl.BlockSpec((rows, top), lambda i: (0, 0)),
        pl.BlockSpec((rows, top), lambda i: (0, 0)),
        pl.BlockSpec((chain, tile), lambda i: (0, i)),
    ]
    args = [route_ids, gate_weights, returned]
    aliases = {}
    if mixed is not None:
        in_specs.append(pl.BlockSpec(memory_space=pl.ANY))
        args.append(mixed)
        aliases = {3: 0}
    return pl.pallas_call(
        kernel,
        grid=(steps,),
        in_specs=in_specs,
        out_specs=pl.BlockSpec((rows, tile), lambda i: (0, part * steps + i)),
        out_shape=jax.ShapeDtypeStruct((rows, width * parts), BF16),
        scratch_shapes=[pltpu.VMEM((rows, chain), BF16), pltpu.VMEM((rows, chain), BF16)],
        input_output_aliases=aliases,
        compiler_params=pltpu.CompilerParams(vmem_limit_bytes=VMEM_LIMIT),
        cost_estimate=pl.CostEstimate(
            flops=4 * rows * chain * width,
            bytes_accessed=2 * width * (rows + chain),
            transcendentals=0,
        ),
    )(*args)


def earlier_state(states, axis, head_count):
    size = lax.axis_size(axis)
    place = lax.axis_index(axis)
    total, total_log = states[:head_count], states[head_count, :head_count, 0]
    found = jnp.zeros_like(total)
    found_log = jnp.zeros_like(total_log)
    step = 1
    while step < size:
        last = step * 2 >= size
        if last:
            pairs = [(i, i + step) for i in range(size - step) if not i & step]
        else:
            pairs = [(i, i ^ step) for i in range(size)]
        planes = jnp.concatenate(
            [total, jnp.zeros((1,) + total.shape[1:], F32).at[0, :head_count, :].set(total_log[:, None])]
        ) if step > 1 else states
        other = lax.ppermute(planes, axis, pairs)
        other_total, other_log = other[:head_count], other[head_count, :head_count, 0]
        upper = (place & step) != 0
        found = found + jnp.where(upper, jnp.exp(found_log), 0.0)[:, None, None] * other_total
        found_log = found_log + jnp.where(upper, other_log, 0.0)
        if not last:
            mine = jnp.where(upper, 1.0, jnp.exp(other_log))[:, None, None]
            theirs = jnp.where(upper, jnp.exp(total_log), 1.0)[:, None, None]
            total = mine * total + theirs * other_total
            total_log = total_log + other_log
        step *= 2
    return found


def on_device(tokens, queries, log_decay, route_ids, gate_weights, kv_weight):
    tok_rows, model_width = tokens.shape
    head_count = log_decay.shape[1]
    head_size = model_width // head_count
    top_count = route_ids.shape[1]
    members = lax.axis_size("mem")
    capacity = 3 * tok_rows * top_count // (2 * members)
    chain_rows = members * capacity
    parts = 2
    routes_t = route_ids.T
    decay_t = log_decay.T

    def swap(rows):
        sent = rows.reshape(members, capacity, rows.shape[-1])
        return lax.all_to_all(sent, "mem", split_axis=0, concat_axis=0, tiled=True).reshape(
            rows.shape
        )

    send_tokens, send_decay = dispatch(routes_t, tokens, members, capacity, 1, decay_t)
    received_decay = lax.all_to_all(send_decay, "mem", split_axis=0, concat_axis=0, tiled=True)
    chain_x = swap(send_tokens)
    send_queries = dispatch(routes_t, queries, members, capacity, parts)
    query_parts = [swap(q) for q in send_queries]
    logs = jnp.moveaxis(received_decay, 0, 1).reshape(head_count, chain_rows).astype(F32)
    running = jnp.cumsum(logs, axis=1)
    projected = jnp.dot(chain_x, kv_weight[0], preferred_element_type=F32).astype(BF16)
    states = local_states(projected, running, head_count, head_size)
    incoming = earlier_state(states, "tm", head_count)
    rows = math.gcd(chain_rows, 128)
    heads_part = head_count // parts
    mixed = None
    for p in range(parts):
        normed = chain_outputs(
            query_parts[p], projected, running, incoming, p * heads_part, head_count, head_size, rows
        )
        mixed = combine(
            route_ids, gate_weights, swap(normed), mixed, p, parts, members, capacity
        )
    return mixed


def solution(mesh):
    placed = (
        P(("tm", "mem"), None),
        P(("tm", "mem"), None),
        P(("tm", "mem"), None),
        P(("tm", "mem"), None),
        P(("tm", "mem"), None),
        P("mem", None, None),
    )
    return jax.shard_map(
        on_device, mesh=mesh, in_specs=placed, out_specs=P(("tm", "mem"), None), check_vma=False
    )
```

```python
import math

import jax
import jax.numpy as jnp
from jax import lax
from jax.experimental import pallas as pl
from jax.experimental.pallas import tpu as pltpu
from jax.sharding import PartitionSpec as P

F32 = jnp.float32
BF16 = jnp.bfloat16
VMEM_LIMIT = 40 << 20
LANES = 128
FACT_PAD = 4
HEAD_PARTS = (8, 8)


def mm(a, b):
    return lax.dot_general(a, b, (((1,), (0,)), ((), ())), preferred_element_type=F32)


def mm_nt(a, b):
    return lax.dot_general(a, b, (((1,), (1,)), ((), ())), preferred_element_type=F32)


def split(x):
    high = x.astype(BF16)
    return high, (x - high.astype(F32)).astype(BF16)


def row_slots(routes, members, capacity):
    top, rows = routes.shape
    member = lax.broadcasted_iota(jnp.int32, (members, rows), 0)
    hits = [routes[j : j + 1, :] == member for j in range(top)]
    named = hits[0]
    for hit in hits[1:]:
        named = jnp.logical_or(named, hit)
    source = lax.broadcasted_iota(jnp.int32, (rows, rows), 0)
    target = lax.broadcasted_iota(jnp.int32, (rows, rows), 1)
    earlier = jnp.where(source < target, 1.0, 0.0).astype(BF16)
    before = mm(jnp.where(named, 1.0, 0.0).astype(BF16), earlier)
    slots = []
    for j in range(top):
        place = jnp.sum(jnp.where(hits[j], before, 0.0), axis=0, keepdims=True)
        slots.append(routes[j : j + 1, :] * capacity + place.astype(jnp.int32))
    return slots


def half_slots(facts, half, top, members, capacity):
    rows = facts.shape[1]
    share = members // 2 * capacity
    slots = row_slots(facts[:top, :].astype(jnp.int32), members, capacity)
    index = lax.broadcasted_iota(jnp.int32, (share, rows), 0) + half * share
    return slots, index


SMEM_SPEC = pl.BlockSpec(memory_space=pltpu.SMEM)
VMEM_SPEC = pl.BlockSpec(memory_space=pltpu.VMEM)


def dispatch(half, facts, data, top, members, capacity, heads):
    rows, width = data.shape
    share = members // 2 * capacity
    full = width + (LANES if heads else 0)
    tile = 512

    def kernel(half_ref, facts_ref, data_ref, out_ref):
        slots, index = half_slots(facts_ref[...], half_ref[0], top, members, capacity)
        chosen = index == slots[0]
        for slot in slots[1:]:
            chosen = jnp.logical_or(chosen, index == slot)
        pick = jnp.where(chosen, 1.0, 0.0).astype(BF16)
        for c in range(0, width, tile):
            out_ref[:, c : c + tile] = mm(pick, data_ref[:, c : c + tile]).astype(BF16)
        if heads:
            decay = facts_ref[2 * top + FACT_PAD :, :].astype(BF16)
            decay = jnp.concatenate([decay, jnp.zeros((LANES - heads, rows), BF16)], axis=0)
            out_ref[:, width:] = mm_nt(pick, decay).astype(BF16)

    return pl.pallas_call(
        kernel,
        in_specs=[SMEM_SPEC, VMEM_SPEC, VMEM_SPEC],
        out_specs=VMEM_SPEC,
        out_shape=jax.ShapeDtypeStruct((share, full), BF16),
        compiler_params=pltpu.CompilerParams(vmem_limit_bytes=VMEM_LIMIT),
        cost_estimate=pl.CostEstimate(
            flops=2 * share * rows * width,
            bytes_accessed=2 * width * (rows + share),
            transcendentals=0,
        ),
    )(half, facts, data)


def gate_matrices(half, facts, partner_facts, top, members, capacity):
    rows = facts.shape[1]
    share = members // 2 * capacity

    def kernel(half_ref, facts_ref, partner_ref, high_ref, low_ref):
        for b, ref in enumerate((facts_ref, partner_ref)):
            values = ref[...]
            slots, index = half_slots(values, half_ref[0], top, members, capacity)
            gates = jnp.zeros((share, rows), F32)
            for j in range(top):
                gates = jnp.where(index == slots[j], values[top + j : top + j + 1, :], gates)
            high_ref[b], low_ref[b] = split(gates.T)

    shape = jax.ShapeDtypeStruct((2, rows, share), BF16)
    return pl.pallas_call(
        kernel,
        in_specs=[SMEM_SPEC, VMEM_SPEC, VMEM_SPEC],
        out_specs=[VMEM_SPEC, VMEM_SPEC],
        out_shape=[shape, shape],
        compiler_params=pltpu.CompilerParams(vmem_limit_bytes=VMEM_LIMIT),
        cost_estimate=pl.CostEstimate(
            flops=4 * rows * rows * members,
            bytes_accessed=8 * rows * share,
            transcendentals=0,
        ),
    )(half, facts, partner_facts)


def project(rows_in, weight):
    share = rows_in.shape[0]
    depth, width = weight.shape
    tile = 512

    def kernel(rows_ref, weight_ref, out_ref):
        out_ref[...] = mm(rows_ref[...], weight_ref[...]).astype(BF16)

    return pl.pallas_call(
        kernel,
        grid=(width // tile,),
        in_specs=[
            pl.BlockSpec((share, depth), lambda i: (0, 0)),
            pl.BlockSpec((depth, tile), lambda i: (0, i)),
        ],
        out_specs=pl.BlockSpec((share, tile), lambda i: (0, i)),
        out_shape=jax.ShapeDtypeStruct((share, width), BF16),
        compiler_params=pltpu.CompilerParams(vmem_limit_bytes=VMEM_LIMIT),
        cost_estimate=pl.CostEstimate(
            flops=2 * share * depth * width,
            bytes_accessed=2 * (share * (depth + width) + depth * width),
            transcendentals=0,
        ),
    )(rows_in, weight)


def local_states(half, near, far, near_rows, far_rows, head_count, head_size):
    share = near.shape[0]
    decay_block = near_rows.shape[1] // LANES - 1

    def kernel(half_ref, nk, nv, fk, fv, near_decay, far_decay, state_ref, running_ref):
        h = pl.program_id(0)
        mine = half_ref[0]

        @pl.when(h == 0)
        def _():
            source = lax.broadcasted_iota(jnp.int32, (share, share), 0)
            target = lax.broadcasted_iota(jnp.int32, (share, share), 1)
            upto = jnp.where(source <= target, 1.0, 0.0).astype(BF16)

            def sums(ref):
                logs = ref[...].astype(F32).T[:head_count, :].astype(BF16)
                return mm(logs, upto)

            running_ref[mine] = sums(near_decay)
            running_ref[1 - mine] = sums(far_decay)
            running_ref[1] = running_ref[1] + running_ref[0][:, share - 1 :]

        @pl.when(h < head_count)
        def _():
            last = running_ref[1, pl.ds(h, 1), :][:, share - 1 :]
            total = None
            for key_ref, value_ref, place in ((nk, nv, mine), (fk, fv, 1 - mine)):
                row = running_ref[place, pl.ds(h, 1), :]
                high, low = split(key_ref[...].T.astype(F32) * jnp.exp(last - row))
                values = value_ref[...]
                term = mm(high, values) + mm(low, values)
                total = term if total is None else total + term
            state_ref[0] = total

        @pl.when(h == head_count)
        def _():
            state_ref[...] = jnp.zeros_like(state_ref)
            state_ref[0, :head_count, :] = jnp.broadcast_to(
                running_ref[1][:, share - 1 :], (head_count, head_size)
            )

    last_head = head_count - 1

    def block(shift):
        return pl.BlockSpec(
            (share, head_size), lambda h: (0, shift + jnp.minimum(h, last_head))
        )

    decay_spec = pl.BlockSpec((share, LANES), lambda h: (0, decay_block))
    return pl.pallas_call(
        kernel,
        grid=(head_count + 1,),
        in_specs=[
            SMEM_SPEC,
            block(0),
            block(head_count),
            block(0),
            block(head_count),
            decay_spec,
            decay_spec,
        ],
        out_specs=[
            pl.BlockSpec((1, head_size, head_size), lambda h: (h, 0, 0)),
            pl.BlockSpec((2, head_count, share), lambda h: (0, 0, 0)),
        ],
        out_shape=[
            jax.ShapeDtypeStruct((head_count + 1, head_size, head_size), F32),
            jax.ShapeDtypeStruct((2, head_count, share), F32),
        ],
        compiler_params=pltpu.CompilerParams(vmem_limit_bytes=VMEM_LIMIT),
        cost_estimate=pl.CostEstimate(
            flops=8 * share * head_size * head_size * head_count,
            bytes_accessed=near.size * 4 + head_count * head_size * head_size * 4,
            transcendentals=2 * share * head_count,
        ),
    )(half, near, near, far, far, near_rows, far_rows)


def chain_outputs(half, near_q, far_q, near, far, running, incoming, first_head, here, head_count, head_size, capacity, rows):
    share = near.shape[0]
    group = share // capacity

    def kernel(half_ref, nq, fq, nk, fk, nv, fv, running_ref, incoming_ref, out_ref, q_s, k_s, v_s, o_s):
        h = pl.program_id(0) + first_head
        mine = half_ref[0]
        for scratch, near_ref, far_ref in ((q_s, nq, fq), (k_s, nk, fk), (v_s, nv, fv)):
            scratch[mine] = near_ref[...]
            scratch[1 - mine] = far_ref[...]
        state = incoming_ref[0]
        up = lax.broadcasted_iota(jnp.int32, (rows, rows), 0)
        across = lax.broadcasted_iota(jnp.int32, (rows, rows), 1)
        lower = up >= across
        previous = jnp.zeros((1, 1), F32)
        for side in range(2):
            running_row = running_ref[side, pl.ds(h, 1), :]
            for c in range(share // rows):
                span = slice(c * rows, (c + 1) * rows)
                query, key, value = q_s[side, span, :], k_s[side, span, :], v_s[side, span, :]
                row = running_row[:, span]
                wide = jnp.broadcast_to(row, (rows, rows))
                tall = wide.T
                weights = jnp.where(lower, jnp.exp(jnp.minimum(tall - wide, 0.0)), 0.0)
                scores, scores_low = split(mm_nt(query, key) * weights)
                state_high, state_low = split(state)
                grown = jnp.exp(tall[:, :head_size] - previous)
                earlier = (mm(query, state_high) + mm(query, state_low)) * grown
                outputs = mm(scores, value) + mm(scores_low, value) + earlier
                mean_square = jnp.mean(outputs * outputs, axis=-1, keepdims=True)
                o_s[side, span, :] = (outputs * lax.rsqrt(mean_square + 1e-06)).astype(BF16)
                ending = row[:, rows - 1 :]
                if side == 0 or (c + 1) * rows < share:
                    faded, faded_low = split(key.T.astype(F32) * jnp.exp(ending - row))
                    state = (
                        jnp.exp(ending - previous) * state
                        + mm(faded, value)
                        + mm(faded_low, value)
                    )
                previous = ending
        for b, place in enumerate((mine, 1 - mine)):
            for k in range(group):
                out_ref[k, b] = o_s[place, k * capacity : (k + 1) * capacity, :]

    def block(shift):
        return pl.BlockSpec((share, head_size), lambda h: (0, shift + first_head + h))

    return pl.pallas_call(
        kernel,
        grid=(here,),
        in_specs=[
            SMEM_SPEC,
            block(0),
            block(0),
            block(0),
            block(0),
            block(head_count),
            block(head_count),
            pl.BlockSpec(running.shape, lambda h: (0, 0, 0)),
            pl.BlockSpec((1, head_size, head_size), lambda h: (first_head + h, 0, 0)),
        ],
        out_specs=pl.BlockSpec((group, 2, capacity, head_size), lambda h: (0, 0, 0, h)),
        out_shape=jax.ShapeDtypeStruct((group, 2, capacity, here * head_size), BF16),
        scratch_shapes=[pltpu.VMEM((2, share, head_size), BF16) for _ in range(4)],
        compiler_params=pltpu.CompilerParams(vmem_limit_bytes=VMEM_LIMIT),
        cost_estimate=pl.CostEstimate(
            flops=2 * here * share * head_size * (6 * rows + 8 * head_size),
            bytes_accessed=16 * share * here * head_size,
            transcendentals=2 * here * share * rows,
        ),
    )(half, near_q, far_q, near, far, near, far, running, incoming)


def partner_sums(high, low, returned):
    group, _, capacity, width = returned.shape
    rows, share = high.shape[1:]
    tile = min(512, width)

    def kernel(high_ref, low_ref, returned_ref, out_ref):
        data = returned_ref[...].reshape(share, tile)
        out_ref[...] = (mm(high_ref[...], data) + mm(low_ref[...], data)).astype(BF16)

    gates = pl.BlockSpec((None, rows, share), lambda i: (1, 0, 0))
    return pl.pallas_call(
        kernel,
        grid=(width // tile,),
        in_specs=[
            gates,
            gates,
            pl.BlockSpec((group, None, capacity, tile), lambda i: (0, 1, 0, i)),
        ],
        out_specs=pl.BlockSpec((rows, tile), lambda i: (0, i)),
        out_shape=jax.ShapeDtypeStruct((rows, width), BF16),
        compiler_params=pltpu.CompilerParams(vmem_limit_bytes=VMEM_LIMIT),
        cost_estimate=pl.CostEstimate(
            flops=4 * rows * share * width,
            bytes_accessed=2 * width * (rows + share),
            transcendentals=0,
        ),
    )(high, low, returned)


def finish(high, low, returned, partner, mixed, first_column, full_width):
    group, _, capacity, width = returned.shape
    rows, share = high.shape[1:]
    tile = min(512, width)
    first = first_column // tile

    def kernel(*refs):
        high_ref, low_ref, returned_ref, partner_ref = refs[:4]
        data = returned_ref[...].reshape(share, tile)
        total = mm(high_ref[...], data) + mm(low_ref[...], data)
        refs[-1][...] = (total + partner_ref[...].astype(F32)).astype(BF16)

    gates = pl.BlockSpec((None, rows, share), lambda i: (0, 0, 0))
    in_specs = [
        gates,
        gates,
        pl.BlockSpec((group, None, capacity, tile), lambda i: (0, 0, 0, i)),
        pl.BlockSpec((rows, tile), lambda i: (0, i)),
    ]
    args = [high, low, returned, partner]
    aliases = {}
    if mixed is not None:
        in_specs.append(pl.BlockSpec(memory_space=pl.ANY))
        args.append(mixed)
        aliases = {4: 0}
    return pl.pallas_call(
        kernel,
        grid=(width // tile,),
        in_specs=in_specs,
        out_specs=pl.BlockSpec((rows, tile), lambda i: (0, first + i)),
        out_shape=jax.ShapeDtypeStruct((rows, full_width), BF16),
        input_output_aliases=aliases,
        compiler_params=pltpu.CompilerParams(vmem_limit_bytes=VMEM_LIMIT),
        cost_estimate=pl.CostEstimate(
            flops=4 * rows * share * width,
            bytes_accessed=2 * width * (2 * rows + share),
            transcendentals=0,
        ),
    )(*args)


def earlier_state(states, axis, head_count):
    size = lax.axis_size(axis)
    place = lax.axis_index(axis)
    total, total_log = states[:head_count], states[head_count, :head_count, 0]
    found = jnp.zeros_like(total)
    found_log = jnp.zeros_like(total_log)
    step = 1
    while step < size:
        last = step * 2 >= size
        if last:
            pairs = [(i, i + step) for i in range(size - step) if not i & step]
        else:
            pairs = [(i, i ^ step) for i in range(size)]
        planes = jnp.concatenate(
            [total, jnp.zeros((1,) + total.shape[1:], F32).at[0, :head_count, :].set(total_log[:, None])]
        ) if step > 1 else states
        other = lax.ppermute(planes, axis, pairs)
        other_total, other_log = other[:head_count], other[head_count, :head_count, 0]
        upper = (place & step) != 0
        found = found + jnp.where(upper, jnp.exp(found_log), 0.0)[:, None, None] * other_total
        found_log = found_log + jnp.where(upper, other_log, 0.0)
        if not last:
            mine = jnp.where(upper, 1.0, jnp.exp(other_log))[:, None, None]
            theirs = jnp.where(upper, jnp.exp(total_log), 1.0)[:, None, None]
            total = mine * total + theirs * other_total
            total_log = total_log + other_log
        step *= 2
    return found


def on_device(tokens, queries, log_decay, route_ids, gate_weights, kv_weight):
    tok_rows, model_width = tokens.shape
    head_count = log_decay.shape[1]
    head_size = model_width // head_count
    top = route_ids.shape[1]
    members = lax.axis_size("mem")
    capacity = 3 * tok_rows * top // (2 * members)
    group = members // 2
    share = group * capacity
    rows = math.gcd(share, 128)
    half = (lax.axis_index("mem") // group).astype(jnp.int32).reshape(1)
    across = [(i, (i + group) % members) for i in range(members)]
    sides = [list(range(group)), list(range(group, members))]

    def cross(array):
        return lax.ppermute(array, "mem", across)

    def swap(array):
        sent = array.reshape((group, -1) + array.shape[1:] if array.ndim == 2 else array.shape)
        return lax.all_to_all(
            sent, "mem", split_axis=0, concat_axis=0, axis_index_groups=sides, tiled=True
        ).reshape(array.shape)

    facts = jnp.concatenate(
        [
            route_ids.T.astype(F32),
            gate_weights.T,
            jnp.zeros((FACT_PAD, tok_rows), F32),
            log_decay.T.astype(F32),
        ],
        axis=0,
    )
    far_facts = cross(facts)
    far_tokens = cross(tokens)
    near_rows = swap(dispatch(half, facts, tokens, top, members, capacity, head_count))
    near = project(near_rows, kv_weight[0])
    far_rows = swap(dispatch(half, far_facts, far_tokens, top, members, capacity, head_count))
    later_queries, far_tokens = lax.optimization_barrier((queries, far_tokens))
    far_queries = cross(later_queries)
    near_q = dispatch(half, facts, queries, top, members, capacity, 0)
    near_q, far_rows = lax.optimization_barrier((near_q, far_rows))
    near_q = swap(near_q)
    far = project(far_rows, kv_weight[0])
    states, running = local_states(half, near, far, near_rows, far_rows, head_count, head_size)
    incoming = earlier_state(states, "tm", head_count)
    high, low = gate_matrices(half, facts, far_facts, top, members, capacity)
    far_q = swap(dispatch(half, far_facts, far_queries, top, members, capacity, 0))
    mixed = None
    first = 0
    for here in HEAD_PARTS:
        normed = chain_outputs(
            half, near_q, far_q, near, far, running, incoming,
            first, here, head_count, head_size, capacity, rows,
        )
        returned = swap(normed)
        partner = cross(partner_sums(high, low, returned))
        mixed = finish(high, low, returned, partner, mixed, first * head_size, model_width)
        first += here
    return mixed


def solution(mesh):
    placed = (
        P(("tm", "mem"), None),
        P(("tm", "mem"), None),
        P(("tm", "mem"), None),
        P(("tm", "mem"), None),
        P(("tm", "mem"), None),
        P("mem", None, None),
    )
    return jax.shard_map(
        on_device, mesh=mesh, in_specs=placed, out_specs=P(("tm", "mem"), None), check_vma=False
    )
```

```python
import math

import jax
import jax.numpy as jnp
from jax import lax
from jax.experimental import pallas as pl
from jax.experimental.pallas import tpu as pltpu
from jax.sharding import PartitionSpec as P


F32 = jnp.float32
BF16 = jnp.bfloat16
LANES = 128
FACT_PAD = 4
HEAD_PARTS = (8, 8)


def mm(a, b):
    return lax.dot_general(a, b, (((1,), (0,)), ((), ())), preferred_element_type=F32)


def mm_nt(a, b):
    return lax.dot_general(a, b, (((1,), (1,)), ((), ())), preferred_element_type=F32)


def split(x):
    high = x.astype(BF16)
    return high, (x - high.astype(F32)).astype(BF16)


def row_slots(routes, members, capacity):
    top, rows = routes.shape
    member = lax.broadcasted_iota(jnp.int32, (members, rows), 0)
    hits = [routes[j : j + 1, :] == member for j in range(top)]
    named = hits[0]
    for hit in hits[1:]:
        named = jnp.logical_or(named, hit)
    source = lax.broadcasted_iota(jnp.int32, (rows, rows), 0)
    target = lax.broadcasted_iota(jnp.int32, (rows, rows), 1)
    earlier = jnp.where(source < target, 1.0, 0.0).astype(BF16)
    before = mm(jnp.where(named, 1.0, 0.0).astype(BF16), earlier)
    slots = []
    for j in range(top):
        place = jnp.sum(jnp.where(hits[j], before, 0.0), axis=0, keepdims=True)
        slots.append(routes[j : j + 1, :] * capacity + place.astype(jnp.int32))
    return slots


def half_slots(facts, half, top, members, capacity):
    rows = facts.shape[1]
    share = members // 2 * capacity
    slots = row_slots(facts[:top, :].astype(jnp.int32), members, capacity)
    index = lax.broadcasted_iota(jnp.int32, (share, rows), 0) + half * share
    return slots, index


SMEM_SPEC = pl.BlockSpec(memory_space=pltpu.SMEM)
VMEM_SPEC = pl.BlockSpec(memory_space=pltpu.VMEM)


def dispatch(half, facts, data, top, members, capacity, heads):
    rows, width = data.shape
    share = members // 2 * capacity
    full = width + (LANES if heads else 0)
    tile = 512

    def kernel(half_ref, facts_ref, data_ref, out_ref):
        slots, index = half_slots(facts_ref[...], half_ref[0], top, members, capacity)
        chosen = index == slots[0]
        for slot in slots[1:]:
            chosen = jnp.logical_or(chosen, index == slot)
        pick = jnp.where(chosen, 1.0, 0.0).astype(BF16)
        for c in range(0, width, tile):
            out_ref[:, c : c + tile] = mm(pick, data_ref[:, c : c + tile]).astype(BF16)
        if heads:
            decay = facts_ref[2 * top + FACT_PAD :, :].astype(BF16)
            decay = jnp.concatenate([decay, jnp.zeros((LANES - heads, rows), BF16)], axis=0)
            out_ref[:, width:] = mm_nt(pick, decay).astype(BF16)

    return pl.pallas_call(
        kernel,
        in_specs=[SMEM_SPEC, VMEM_SPEC, VMEM_SPEC],
        out_specs=VMEM_SPEC,
        out_shape=jax.ShapeDtypeStruct((share, full), BF16),
        cost_estimate=pl.CostEstimate(
            flops=2 * share * rows * width,
            bytes_accessed=2 * width * (rows + share),
            transcendentals=0,
        ),
    )(half, facts, data)


def gate_matrices(half, facts, partner_facts, top, members, capacity):
    rows = facts.shape[1]
    share = members // 2 * capacity

    def kernel(half_ref, facts_ref, partner_ref, high_ref, low_ref):
        for b, ref in enumerate((facts_ref, partner_ref)):
            values = ref[...]
            slots, index = half_slots(values, half_ref[0], top, members, capacity)
            gates = jnp.zeros((share, rows), F32)
            for j in range(top):
                gates = jnp.where(index == slots[j], values[top + j : top + j + 1, :], gates)
            high_ref[b], low_ref[b] = split(gates.T)

    shape = jax.ShapeDtypeStruct((2, rows, share), BF16)
    return pl.pallas_call(
        kernel,
        in_specs=[SMEM_SPEC, VMEM_SPEC, VMEM_SPEC],
        out_specs=[VMEM_SPEC, VMEM_SPEC],
        out_shape=[shape, shape],
        cost_estimate=pl.CostEstimate(
            flops=4 * rows * rows * members,
            bytes_accessed=8 * rows * share,
            transcendentals=0,
        ),
    )(half, facts, partner_facts)


def project(rows_in, weight):
    share = rows_in.shape[0]
    depth, width = weight.shape
    tile = 512

    def kernel(rows_ref, weight_ref, out_ref):
        out_ref[...] = mm(rows_ref[...], weight_ref[...]).astype(BF16)

    return pl.pallas_call(
        kernel,
        grid=(width // tile,),
        in_specs=[
            pl.BlockSpec((share, depth), lambda i: (0, 0)),
            pl.BlockSpec((depth, tile), lambda i: (0, i)),
        ],
        out_specs=pl.BlockSpec((share, tile), lambda i: (0, i)),
        out_shape=jax.ShapeDtypeStruct((share, width), BF16),
        cost_estimate=pl.CostEstimate(
            flops=2 * share * depth * width,
            bytes_accessed=2 * (share * (depth + width) + depth * width),
            transcendentals=0,
        ),
    )(rows_in, weight)


def local_states(half, near, far, near_rows, far_rows, head_count, head_size):
    share = near.shape[0]
    decay_block = near_rows.shape[1] // LANES - 1

    def kernel(half_ref, nk, nv, fk, fv, near_decay, far_decay, state_ref, running_ref):
        h = pl.program_id(0)
        mine = half_ref[0]

        @pl.when(h == 0)
        def _():
            source = lax.broadcasted_iota(jnp.int32, (share, share), 0)
            target = lax.broadcasted_iota(jnp.int32, (share, share), 1)
            upto = jnp.where(source <= target, 1.0, 0.0).astype(BF16)

            def sums(ref):
                logs = ref[...].astype(F32).T[:head_count, :].astype(BF16)
                return mm(logs, upto)

            running_ref[mine] = sums(near_decay)
            running_ref[1 - mine] = sums(far_decay)
            running_ref[1] = running_ref[1] + running_ref[0][:, share - 1 :]

        @pl.when(h < head_count)
        def _():
            last = running_ref[1, pl.ds(h, 1), :][:, share - 1 :]
            total = None
            for key_ref, value_ref, place in ((nk, nv, mine), (fk, fv, 1 - mine)):
                row = running_ref[place, pl.ds(h, 1), :]
                high, low = split(key_ref[...].T.astype(F32) * jnp.exp(last - row))
                values = value_ref[...]
                term = mm(high, values) + mm(low, values)
                total = term if total is None else total + term
            state_ref[0] = total

        @pl.when(h == head_count)
        def _():
            state_ref[...] = jnp.zeros_like(state_ref)
            state_ref[0, :head_count, :] = jnp.broadcast_to(
                running_ref[1][:, share - 1 :], (head_count, head_size)
            )

    last_head = head_count - 1

    def block(shift):
        return pl.BlockSpec(
            (share, head_size), lambda h: (0, shift + jnp.minimum(h, last_head))
        )

    decay_spec = pl.BlockSpec((share, LANES), lambda h: (0, decay_block))
    return pl.pallas_call(
        kernel,
        grid=(head_count + 1,),
        in_specs=[
            SMEM_SPEC,
            block(0),
            block(head_count),
            block(0),
            block(head_count),
            decay_spec,
            decay_spec,
        ],
        out_specs=[
            pl.BlockSpec((1, head_size, head_size), lambda h: (h, 0, 0)),
            pl.BlockSpec((2, head_count, share), lambda h: (0, 0, 0)),
        ],
        out_shape=[
            jax.ShapeDtypeStruct((head_count + 1, head_size, head_size), F32),
            jax.ShapeDtypeStruct((2, head_count, share), F32),
        ],
        cost_estimate=pl.CostEstimate(
            flops=8 * share * head_size * head_size * head_count,
            bytes_accessed=near.size * 4 + head_count * head_size * head_size * 4,
            transcendentals=2 * share * head_count,
        ),
    )(half, near, near, far, far, near_rows, far_rows)


def chain_outputs(half, near_q, far_q, near, far, running, incoming, first_head, here, head_count, head_size, capacity, rows):
    share = near.shape[0]
    group = share // capacity

    def kernel(half_ref, nq, fq, nk, fk, nv, fv, running_ref, incoming_ref, out_ref, q_s, k_s, v_s, o_s):
        h = pl.program_id(0) + first_head
        mine = half_ref[0]
        for scratch, near_ref, far_ref in ((q_s, nq, fq), (k_s, nk, fk), (v_s, nv, fv)):
            scratch[mine] = near_ref[...]
            scratch[1 - mine] = far_ref[...]
        state = incoming_ref[0]
        up = lax.broadcasted_iota(jnp.int32, (rows, rows), 0)
        across = lax.broadcasted_iota(jnp.int32, (rows, rows), 1)
        lower = up >= across
        previous = jnp.zeros((1, 1), F32)
        for side in range(2):
            running_row = running_ref[side, pl.ds(h, 1), :]
            for c in range(share // rows):
                span = slice(c * rows, (c + 1) * rows)
                query, key, value = q_s[side, span, :], k_s[side, span, :], v_s[side, span, :]
                row = running_row[:, span]
                wide = jnp.broadcast_to(row, (rows, rows))
                tall = wide.T
                weights = jnp.where(lower, jnp.exp(jnp.minimum(tall - wide, 0.0)), 0.0)
                scores, scores_low = split(mm_nt(query, key) * weights)
                state_high, state_low = split(state)
                grown = jnp.exp(tall[:, :head_size] - previous)
                earlier = (mm(query, state_high) + mm(query, state_low)) * grown
                outputs = mm(scores, value) + mm(scores_low, value) + earlier
                mean_square = jnp.mean(outputs * outputs, axis=-1, keepdims=True)
                o_s[side, span, :] = (outputs * lax.rsqrt(mean_square + 1e-06)).astype(BF16)
                ending = row[:, rows - 1 :]
                if side == 0 or (c + 1) * rows < share:
                    faded, faded_low = split(key.T.astype(F32) * jnp.exp(ending - row))
                    state = (
                        jnp.exp(ending - previous) * state
                        + mm(faded, value)
                        + mm(faded_low, value)
                    )
                previous = ending
        for b, place in enumerate((mine, 1 - mine)):
            for k in range(group):
                out_ref[k, b] = o_s[place, k * capacity : (k + 1) * capacity, :]

    def block(shift):
        return pl.BlockSpec((share, head_size), lambda h: (0, shift + first_head + h))

    return pl.pallas_call(
        kernel,
        grid=(here,),
        in_specs=[
            SMEM_SPEC,
            block(0),
            block(0),
            block(0),
            block(0),
            block(head_count),
            block(head_count),
            pl.BlockSpec(running.shape, lambda h: (0, 0, 0)),
            pl.BlockSpec((1, head_size, head_size), lambda h: (first_head + h, 0, 0)),
        ],
        out_specs=pl.BlockSpec((group, 2, capacity, head_size), lambda h: (0, 0, 0, h)),
        out_shape=jax.ShapeDtypeStruct((group, 2, capacity, here * head_size), BF16),
        scratch_shapes=[pltpu.VMEM((2, share, head_size), BF16) for _ in range(4)],
        cost_estimate=pl.CostEstimate(
            flops=2 * here * share * head_size * (6 * rows + 8 * head_size),
            bytes_accessed=16 * share * here * head_size,
            transcendentals=2 * here * share * rows,
        ),
    )(half, near_q, far_q, near, far, near, far, running, incoming)


def partner_sums(high, low, returned):
    group, _, capacity, width = returned.shape
    rows, share = high.shape[1:]
    tile = min(512, width)

    def kernel(high_ref, low_ref, returned_ref, out_ref):
        data = returned_ref[...].reshape(share, tile)
        out_ref[...] = (mm(high_ref[...], data) + mm(low_ref[...], data)).astype(BF16)

    gates = pl.BlockSpec((None, rows, share), lambda i: (1, 0, 0))
    return pl.pallas_call(
        kernel,
        grid=(width // tile,),
        in_specs=[
            gates,
            gates,
            pl.BlockSpec((group, None, capacity, tile), lambda i: (0, 1, 0, i)),
        ],
        out_specs=pl.BlockSpec((rows, tile), lambda i: (0, i)),
        out_shape=jax.ShapeDtypeStruct((rows, width), BF16),
        cost_estimate=pl.CostEstimate(
            flops=4 * rows * share * width,
            bytes_accessed=2 * width * (rows + share),
            transcendentals=0,
        ),
    )(high, low, returned)


def finish(high, low, returned, partner, mixed, first_column, full_width):
    group, _, capacity, width = returned.shape
    rows, share = high.shape[1:]
    tile = min(512, width)
    first = first_column // tile

    def kernel(*refs):
        high_ref, low_ref, returned_ref, partner_ref = refs[:4]
        data = returned_ref[...].reshape(share, tile)
        total = mm(high_ref[...], data) + mm(low_ref[...], data)
        refs[-1][...] = (total + partner_ref[...].astype(F32)).astype(BF16)

    gates = pl.BlockSpec((None, rows, share), lambda i: (0, 0, 0))
    in_specs = [
        gates,
        gates,
        pl.BlockSpec((group, None, capacity, tile), lambda i: (0, 0, 0, i)),
        pl.BlockSpec((rows, tile), lambda i: (0, i)),
    ]
    args = [high, low, returned, partner]
    aliases = {}
    if mixed is not None:
        in_specs.append(pl.BlockSpec(memory_space=pl.ANY))
        args.append(mixed)
        aliases = {4: 0}
    return pl.pallas_call(
        kernel,
        grid=(width // tile,),
        in_specs=in_specs,
        out_specs=pl.BlockSpec((rows, tile), lambda i: (0, first + i)),
        out_shape=jax.ShapeDtypeStruct((rows, full_width), BF16),
        input_output_aliases=aliases,
        cost_estimate=pl.CostEstimate(
            flops=4 * rows * share * width,
            bytes_accessed=2 * width * (2 * rows + share),
            transcendentals=0,
        ),
    )(*args)


def earlier_state(states, axis, head_count):
    size = lax.axis_size(axis)
    place = lax.axis_index(axis)
    total, total_log = states[:head_count], states[head_count, :head_count, 0]
    found = jnp.zeros_like(total)
    found_log = jnp.zeros_like(total_log)
    step = 1
    while step < size:
        last = step * 2 >= size
        if last:
            pairs = [(i, i + step) for i in range(size - step) if not i & step]
        else:
            pairs = [(i, i ^ step) for i in range(size)]
        planes = jnp.concatenate(
            [total, jnp.zeros((1,) + total.shape[1:], F32).at[0, :head_count, :].set(total_log[:, None])]
        ) if step > 1 else states
        other = lax.ppermute(planes, axis, pairs)
        other_total, other_log = other[:head_count], other[head_count, :head_count, 0]
        upper = (place & step) != 0
        found = found + jnp.where(upper, jnp.exp(found_log), 0.0)[:, None, None] * other_total
        found_log = found_log + jnp.where(upper, other_log, 0.0)
        if not last:
            mine = jnp.where(upper, 1.0, jnp.exp(other_log))[:, None, None]
            theirs = jnp.where(upper, jnp.exp(total_log), 1.0)[:, None, None]
            total = mine * total + theirs * other_total
            total_log = total_log + other_log
        step *= 2
    return found


def on_device(tokens, queries, log_decay, route_ids, gate_weights, kv_weight):
    tok_rows, model_width = tokens.shape
    head_count = log_decay.shape[1]
    head_size = model_width // head_count
    top = route_ids.shape[1]
    members = lax.axis_size("mem")
    capacity = 3 * tok_rows * top // (2 * members)
    group = members // 2
    share = group * capacity
    rows = math.gcd(share, 128)
    half = (lax.axis_index("mem") // group).astype(jnp.int32).reshape(1)
    across = [(i, (i + group) % members) for i in range(members)]
    sides = [list(range(group)), list(range(group, members))]

    def cross(array):
        return lax.ppermute(array, "mem", across)

    def swap(array):
        sent = array.reshape((group, -1) + array.shape[1:] if array.ndim == 2 else array.shape)
        return lax.all_to_all(
            sent, "mem", split_axis=0, concat_axis=0, axis_index_groups=sides, tiled=True
        ).reshape(array.shape)

    facts = jnp.concatenate(
        [
            route_ids.T.astype(F32),
            gate_weights.T,
            jnp.zeros((FACT_PAD, tok_rows), F32),
            log_decay.T.astype(F32),
        ],
        axis=0,
    )
    sizes = (top, members, capacity)
    far_facts = cross(facts)
    far_tokens = cross(tokens)
    near_rows = swap(dispatch(half, facts, tokens, *sizes, head_count))
    near = project(near_rows, kv_weight[0])
    far_rows = swap(dispatch(half, far_facts, far_tokens, *sizes, head_count))
    far_queries = cross(queries)
    near_q = swap(dispatch(half, facts, queries, *sizes, 0))
    far = project(far_rows, kv_weight[0])
    states, running = local_states(half, near, far, near_rows, far_rows, head_count, head_size)
    incoming = earlier_state(states, "tm", head_count)
    high, low = gate_matrices(half, facts, far_facts, *sizes)
    far_q = swap(dispatch(half, far_facts, far_queries, *sizes, 0))
    mixed = None
    first = 0
    for here in HEAD_PARTS:
        normed = chain_outputs(
            half, near_q, far_q, near, far, running, incoming,
            first, here, head_count, head_size, capacity, rows,
        )
        returned = swap(normed)
        partner = cross(partner_sums(high, low, returned))
        mixed = finish(high, low, returned, partner, mixed, first * head_size, model_width)
        first += here
    return mixed


def solution(mesh):
    placed = (
        P(("tm", "mem"), None),
        P(("tm", "mem"), None),
        P(("tm", "mem"), None),
        P(("tm", "mem"), None),
        P(("tm", "mem"), None),
        P("mem", None, None),
    )

    return jax.shard_map(
        on_device, mesh=mesh, in_specs=placed, out_specs=P(("tm", "mem"), None), check_vma=False
    )
```
